32 devices in a mesh: dp: 8 (over y, x, core), mp: 4 (over z).
Axes of the slice: x: 2, y: 2, z: 4, core: 2. Of those that a mesh axis runs over, the one named last changes fastest.
Arguments:
- hidden: float32 [4, 1024, 1024], P('mp', 'dp'), may hold values from -6 to 6
- documents: int32 [4, 1024], P('mp', 'dp'), may hold values from 0 to 3, as said below
- positions: int32 [4, 1024], P('mp', 'dp'), may hold values from 0 to 639, as said below
- w_query: bfloat16 [2, 1024, 1024], P(None, ('dp', 'mp')), may hold values from -0.1875 to 0.1875
- w_key: bfloat16 [2, 1024, 1024], P(None, ('dp', 'mp')), may hold values from -0.1875 to 0.1875
- w_value: bfloat16 [2, 1024, 1024], P(None, ('dp', 'mp')), may hold values from -0.1875 to 0.1875
- w_out: bfloat16 [2, 1024, 1024], P(None, ('dp', 'mp')), may hold values from -0.1875 to 0.1875
- qk_scale: float32 [2, 1024], replicated, may hold values from 0.8 to 1.5
- attn_rate: float32 [2, 1024], replicated, may hold values from 0.15 to 0.6
- mlp_rate: float32 [2, 1024], replicated, may hold values from 0.15 to 0.6
- w_up: bfloat16 [2, 1024, 4096], P(None, None, 'mp'), may hold values from -0.1875 to 0.1875
- w_gate: bfloat16 [2, 1024, 4096], P(None, None, 'mp'), may hold values from -0.1875 to 0.1875
- w_down: bfloat16 [2, 4096, 1024], P(None, 'mp'), may hold values from -0.09375 to 0.09375
- up_scale: float32 [2, 4096], replicated, may hold values from 0.5 to 2
- gate_scale: float32 [2, 4096], replicated, may hold values from 0.5 to 2
- out_grad: float32 [4, 1024, 1024], P('mp', 'dp'), may hold values from -6 to 6
Outputs:
- output: float32 [4, 1024, 1024], P('mp', 'dp')
- input_grad: float32 [4, 1024, 1024], P('mp', 'dp')
- query_grad: float32 [2, 1024, 1024], P(None, ('dp', 'mp'))
- key_grad: float32 [2, 1024, 1024], P(None, ('dp', 'mp'))
- value_grad: float32 [2, 1024, 1024], P(None, ('dp', 'mp'))
- out_proj_grad: float32 [2, 1024, 1024], P(None, ('dp', 'mp'))
- qk_scale_grad: float32 [2, 1024], replicated
- attn_rate_grad: float32 [2, 1024], replicated
- mlp_rate_grad: float32 [2, 1024], replicated
- up_grad: float32 [2, 1024, 4096], P(None, 'dp', 'mp')
- gate_grad: float32 [2, 1024, 4096], P(None, 'dp', 'mp')
- down_grad: float32 [2, 4096, 1024], P(None, 'mp', 'dp')
- up_scale_grad: float32 [2, 4096], replicated
- gate_scale_grad: float32 [2, 4096], replicated
The draws below stay inside these ranges and needn't reach their ends.
Inputs may be any that keep to these rules, and one draw needn't show every extreme that they name: Each row holds 4 documents of consecutive tokens numbered 0 to 3 in order, each at least one token long; one of them is exactly 640 tokens long. `positions`: A token's index within its document, 0 at the document's first token.
All inputs are finite; a program needn't handle non-finite values.
Results may differ from the reference program's by a relative error of at most 0.035.
Values may be sent and summed in bfloat16 or wider, within the bound.
No kernel may reach another device: no remote copies, remote signals or barrier semaphores. Data moves between devices by JAX's collectives and lax.ppermute only.
A program may use at most 320 MiB of HBM per device.

```python
import math
import jax
import jax.numpy as jnp
from jax import lax

D = 1024
HEADS = 16
HEAD_DIM = 64
FF = 4096
LAYERS = 2
SEQ = 1024
ROWS = 4
DOC_LONG = 640


def doc_layout(key):
    base_key = jax.random.fold_in(key, 7)
    row_keys = jax.random.split(base_key, ROWS)

    def one_row(row_key):
        key_one, key_two, key_three = jax.random.split(row_key, 3)
        remain = SEQ - DOC_LONG
        first_cut = jax.random.randint(key_one, (), 1, remain // 2 + 1)
        second_cut = jax.random.randint(key_two, (), remain // 2 + 1, remain)
        others = jnp.stack([first_cut, second_cut - first_cut, remain - second_cut]).astype(jnp.int32)
        long_slot = jax.random.randint(key_three, (), 0, 4)
        slots = jnp.arange(4, dtype=jnp.int32)
        other_index = jnp.clip(slots - (slots > long_slot).astype(jnp.int32), 0, 2)
        lengths = jnp.where(slots == long_slot, DOC_LONG, others[other_index]).astype(jnp.int32)
        ends = jnp.cumsum(lengths).astype(jnp.int32)
        starts = ends - lengths
        places = jnp.arange(SEQ, dtype=jnp.int32)
        doc_row = jnp.sum((places[:, None] >= ends[None, :3]).astype(jnp.int32), axis=1).astype(jnp.int32)
        pos_row = places - starts[doc_row]
        return (doc_row, pos_row.astype(jnp.int32))
    return jax.vmap(one_row)(row_keys)


def draw_documents(key, part):
    return doc_layout(key)[0]


def draw_positions(key, part):
    return doc_layout(key)[1]


def strengthened(result, own_key, source, target, shards_of, factor):
    def block_of(dim):
        return (jnp.arange(result.shape[dim]) // (result.shape[dim] // shards_of)).reshape((-1,) + (1,) * (result.ndim - 1 - dim))

    near = jax.random.permutation(own_key, shards_of)[block_of(target)]
    other_side = (block_of(target) + shards_of // 2) % shards_of
    return jnp.where((block_of(source) == near) | (block_of(source) == other_side), factor * result, result)


def shard_levels(own_key, shape, cuts, low, top_value):
    loudness = 1.0
    for dim, shards_of in cuts:
        steps = jax.random.uniform(jax.random.fold_in(jax.random.fold_in(own_key, 6), dim), (shards_of,), jnp.float32, low / len(cuts), top_value / len(cuts))
        loudness = loudness * jnp.repeat(jnp.exp(steps), shape[dim] // shards_of).reshape((-1,) + (1,) * (len(shape) - 1 - dim))
    return loudness


def bell_draw(own_key, extent, deviation, limit, shards=(), held_as=jnp.bfloat16):
    loudness = shard_levels(own_key, extent, shards, -0.22, 0.18) if shards else 1.0
    result = jax.random.normal(own_key, extent, jnp.float32) * deviation * loudness
    return jnp.minimum(jnp.maximum(result, -limit), limit).astype(held_as)


def heavy_noise(key, shape, scale, reach, cuts, heavy, kind=jnp.bfloat16):
    values = scale * jax.random.normal(key, shape, jnp.float32)
    if cuts:
        values = values * shard_levels(key, shape, cuts, -0.22, 0.18)
    return jnp.clip(strengthened(values, jax.random.fold_in(key, 3), *heavy), -reach, reach).astype(kind)


def setup_inputs(seed: int = 0) -> dict:
    arg_keys = jax.random.split(jax.random.key(seed), 17)
    return {
        "hidden": heavy_noise(arg_keys[0], (ROWS, SEQ, D), 1.0, 6.0, ((0, 4), (1, 8)), (1, 2, 8, 2.0), jnp.float32),
        "documents": draw_documents(jax.random.fold_in(arg_keys[16], 71), 0),
        "positions": draw_positions(jax.random.fold_in(arg_keys[16], 71), 0),
        "w_query": bell_draw(arg_keys[3], (LAYERS, D, D), D ** -0.5, 0.1875, ((1, 32),)),
        "w_key": bell_draw(arg_keys[4], (LAYERS, D, D), D ** -0.5, 0.1875, ((1, 32),)),
        "w_value": bell_draw(arg_keys[5], (LAYERS, D, D), D ** -0.5, 0.1875, ((1, 32),)),
        "w_out": bell_draw(arg_keys[6], (LAYERS, D, D), D ** -0.5, 0.1875, ((1, 32),)),
        "qk_scale": jnp.clip(jnp.exp(jax.random.uniform(arg_keys[7], (LAYERS, D), jnp.float32, math.log(0.8), math.log(1.5))), 0.8, 1.5),
        "attn_rate": jnp.clip(jnp.exp(jax.random.uniform(arg_keys[8], (LAYERS, D), jnp.float32, math.log(0.15), math.log(0.6))), 0.15, 0.6),
        "mlp_rate": jnp.clip(jnp.exp(jax.random.uniform(arg_keys[9], (LAYERS, D), jnp.float32, math.log(0.15), math.log(0.6))), 0.15, 0.6),
        "w_up": bell_draw(arg_keys[10], (LAYERS, D, FF), D ** -0.5, 0.1875, ((2, 4),)),
        "w_gate": bell_draw(arg_keys[11], (LAYERS, D, FF), D ** -0.5, 0.1875, ((2, 4),)),
        "w_down": bell_draw(arg_keys[12], (LAYERS, FF, D), FF ** -0.5, 0.09375, ((1, 4),)),
        "up_scale": jnp.clip(jnp.exp(jax.random.uniform(arg_keys[13], (LAYERS, FF), jnp.float32, math.log(0.5), math.log(2.0))), 0.5, 2.0),
        "gate_scale": jnp.clip(jnp.exp(jax.random.uniform(arg_keys[14], (LAYERS, FF), jnp.float32, math.log(0.5), math.log(2.0))), 0.5, 2.0),
        "out_grad": bell_draw(arg_keys[15], (ROWS, SEQ, D), 1.0, 6.0, ((0, 4), (1, 8)), jnp.float32),
    }


EPS = 1e-06
HIGH = lax.Precision.HIGHEST

@jax.custom_vjp
def low(v):
    return lax.optimization_barrier(v.astype(jnp.bfloat16)).astype(jnp.float32)

@jax.custom_vjp
def low_back(v):
    return v

def low_keep(v):
    return (low(v), None)

def low_pass(kept, grad):
    return (grad,)

def back_keep(v):
    return (v, None)

def back_low(kept, grad):
    return (low(grad),)
low.defvjp(low_keep, low_pass)
low_back.defvjp(back_keep, back_low)

def dot_high(left, right):
    return jnp.dot(left, right, precision=HIGH, preferred_element_type=jnp.float32)

def normed(vector):
    return vector * lax.rsqrt(lax.optimization_barrier(jnp.mean(vector * vector, axis=-1, keepdims=True)) + EPS)

def head_normed(vector):
    row_count = vector.shape[0]
    return normed(vector.reshape(row_count, HEADS, HEAD_DIM)).reshape(row_count, HEADS * HEAD_DIM)

def turn(vector, pos_row):
    row_count = vector.shape[0]
    half_dim = HEAD_DIM // 2
    frequency = jnp.exp(jnp.arange(half_dim, dtype=jnp.float32) * (-2.0 * math.log(10000.0) / HEAD_DIM))
    angles = pos_row.astype(jnp.float32)[:, None] * frequency[None, :]
    cosine = jnp.cos(angles)[:, None, :]
    sine_val = jnp.sin(angles)[:, None, :]
    split = vector.reshape(row_count, HEADS, HEAD_DIM)
    leading = split[..., :half_dim]
    trailing = split[..., half_dim:]
    joined = jnp.concatenate([leading * cosine - trailing * sine_val, trailing * cosine + leading * sine_val], axis=-1)
    return joined.reshape(row_count, HEADS * HEAD_DIM)

def attention_branch(stream, weight_q, weight_k, weight_v, weight_o, qk_factor, doc_row, pos_row):
    row_count = stream.shape[0]
    flat_b16 = low(stream)
    q_raw = low_back(dot_high(flat_b16, weight_q))
    k_raw = low_back(dot_high(flat_b16, weight_k))
    v_raw = low(low_back(dot_high(flat_b16, weight_v)))
    queries = low(qk_factor * head_normed(turn(q_raw, pos_row)))
    key_vals = low(qk_factor * head_normed(turn(k_raw, pos_row)))
    places = jnp.arange(row_count)
    visible = (doc_row[:, None] == doc_row[None, :]) & (places[None, :] <= places[:, None])

    def split_heads(matrix):
        return matrix.reshape(row_count, HEADS, HEAD_DIM).transpose(1, 0, 2)

    def one_head(head_parts):
        query_head, key_head, value_head = head_parts
        scores = low_back(dot_high(query_head, key_head.T) * HEAD_DIM ** (-0.5))
        chances = jax.nn.softmax(jnp.where(visible, scores, -jnp.inf), axis=-1)
        return dot_high(low(chances), value_head)
    mixture = lax.map(jax.checkpoint(one_head), (split_heads(queries), split_heads(key_vals), split_heads(v_raw)))
    mixture = low(low_back(mixture.transpose(1, 0, 2).reshape(row_count, HEADS * HEAD_DIM)))
    return normed(low_back(dot_high(mixture, weight_o)))

def mlp_branch(middle, weight_up, weight_gate, weight_down, factor_up, factor_gate):
    flat_b16 = low(middle)
    up_pre = low_back(dot_high(flat_b16, weight_up))
    gate_pre = low_back(dot_high(flat_b16, weight_gate))
    act_b16 = low(factor_up * up_pre * jax.nn.silu(factor_gate * gate_pre))
    return normed(low_back(dot_high(act_b16, weight_down)))

def reference(hidden, documents, positions, w_query, w_key, w_value, w_out, qk_scale, attn_rate, mlp_rate, w_up, w_gate, w_down, up_scale, gate_scale, out_grad):
    floats = [array_in.astype(jnp.float32) for array_in in (hidden, w_query, w_key, w_value, w_out, qk_scale, attn_rate, mlp_rate, w_up, w_gate, w_down, up_scale, gate_scale)]

    def forward(stream_all, weight_q, weight_k, weight_v, weight_o, qk_factor, rate_attn, rate_mlp, weight_up, weight_gate, weight_down, factor_up, factor_gate):

        def row_pass(row_parts):
            stream, doc_row, pos_row = row_parts
            for layer_no in range(LAYERS):
                branch = attention_branch(stream, weight_q[layer_no], weight_k[layer_no], weight_v[layer_no], weight_o[layer_no], qk_factor[layer_no], doc_row, pos_row)
                middle = normed(stream + rate_attn[layer_no] * (branch - stream))
                mlp_out = mlp_branch(middle, weight_up[layer_no], weight_gate[layer_no], weight_down[layer_no], factor_up[layer_no], factor_gate[layer_no])
                stream = normed(middle + rate_mlp[layer_no] * (mlp_out - middle))
            return stream
        return lax.map(jax.checkpoint(row_pass), (stream_all, documents, positions))
    output, pullback = jax.vjp(forward, *floats)
    gradients = pullback(out_grad.astype(jnp.float32))
    return (output, gradients[0], gradients[1], gradients[2], gradients[3], gradients[4], gradients[5], gradients[6], gradients[7], gradients[8], gradients[9], gradients[10], gradients[11], gradients[12])
```

```python
import math

import jax
import jax.numpy as jnp
from jax import lax
from jax.sharding import PartitionSpec as P

D = 1024
HEADS = 16
HEAD_DIM = 64
FF = 4096
LAYERS = 2


EPS = 1e-06


def normed(vector):
    return vector * lax.rsqrt(jnp.mean(vector * vector, axis=-1, keepdims=True) + EPS)


def norm_back(result, vector, grad_in):
    factor = lax.rsqrt(jnp.mean(vector * vector, axis=-1, keepdims=True) + EPS)
    return factor * (grad_in - result * jnp.mean(result * grad_in, axis=-1, keepdims=True))


def to_heads(matrix):
    return matrix.reshape(matrix.shape[0], HEADS, HEAD_DIM)


def from_heads(tensor):
    return tensor.reshape(tensor.shape[0], HEADS * HEAD_DIM)


def head_normed(vector):
    return from_heads(normed(to_heads(vector)))


def head_norm_back(result, vector, grad_in):
    return from_heads(norm_back(to_heads(result), to_heads(vector), to_heads(grad_in)))


def rotary(pos_row):
    half_dim = HEAD_DIM // 2
    frequency = jnp.exp(
        jnp.arange(half_dim, dtype=jnp.float32) * (-2.0 * math.log(10000.0) / HEAD_DIM)
    )
    angles = pos_row.astype(jnp.float32)[:, None] * frequency[None, :]
    return (jnp.cos(angles)[:, None, :], jnp.sin(angles)[:, None, :])


def turn(vector, cosine, sine_val):
    half_dim = HEAD_DIM // 2
    split = to_heads(vector)
    leading = split[..., :half_dim]
    trailing = split[..., half_dim:]
    return from_heads(
        jnp.concatenate(
            [leading * cosine - trailing * sine_val, trailing * cosine + leading * sine_val],
            axis=-1,
        )
    )


def head_cut(matrix, head_no):
    return lax.dynamic_slice_in_dim(matrix, head_no * HEAD_DIM, HEAD_DIM, 1)


def contract_rows(left, right):
    return lax.dot_general(
        left, right, (((0,), (0,)), ((), ())), preferred_element_type=jnp.float32
    )


def contract_cols(left, right):
    return lax.dot_general(
        left, right, (((1,), (1,)), ((), ())), preferred_element_type=jnp.float32
    )


def head_scores(query_head, key_head, visible):
    scores = jnp.einsum(
        "td,sd->ts", query_head, key_head, preferred_element_type=jnp.float32
    ) * HEAD_DIM ** (-0.5)
    return jnp.where(visible, scores, -jnp.inf)


def softmax_parts(scores):
    maximum = jnp.max(scores, axis=-1, keepdims=True)
    exponent = jnp.exp(scores - maximum)
    summed = jnp.sum(exponent, axis=-1, keepdims=True)
    return (exponent / summed, maximum[:, 0] + jnp.log(summed[:, 0]))


def attend_forward(queries, all_keys, all_values, visible):

    def one_head(head_no):
        chances, log_total = softmax_parts(
            head_scores(head_cut(queries, head_no), head_cut(all_keys, head_no), visible)
        )
        mixture = jnp.dot(
            chances.astype(jnp.bfloat16),
            head_cut(all_values, head_no),
            preferred_element_type=jnp.float32,
        )
        return (mixture, log_total)

    mixture, log_total = lax.map(one_head, jnp.arange(HEADS))
    return (from_heads(mixture.transpose(1, 0, 2)), log_total)


def attend_back(queries, all_keys, all_values, grad_mix, visible):

    def one_head(head_no):
        query_head = head_cut(queries, head_no)
        key_head = head_cut(all_keys, head_no)
        value_head = head_cut(all_values, head_no)
        grad_head = head_cut(grad_mix, head_no)
        chances, log_total = softmax_parts(head_scores(query_head, key_head, visible))
        d_chance = jnp.einsum(
            "td,sd->ts", grad_head, value_head, preferred_element_type=jnp.float32
        )
        row_inner = jnp.sum(chances * d_chance, axis=-1, keepdims=True)
        d_score = (chances * (d_chance - row_inner)).astype(jnp.bfloat16)
        d_query = jnp.dot(d_score, key_head, preferred_element_type=jnp.float32) * HEAD_DIM ** (
            -0.5
        )
        d_key = jnp.einsum(
            "ts,td->sd", d_score, query_head, preferred_element_type=jnp.float32
        ) * HEAD_DIM ** (-0.5)
        d_value = jnp.einsum(
            "ts,td->sd", chances.astype(jnp.bfloat16), grad_head, preferred_element_type=jnp.float32
        )
        return (d_query, d_key, d_value, row_inner[:, 0])

    d_query, d_key, d_value, row_inner = lax.map(one_head, jnp.arange(HEADS))
    return (from_heads(d_query.transpose(1, 0, 2)), d_key, d_value, row_inner)


def per_device(
    hidden,
    documents,
    positions,
    w_query,
    w_key,
    w_value,
    w_out,
    qk_scale,
    attn_rate,
    mlp_rate,
    w_up,
    w_gate,
    w_down,
    up_scale,
    gate_scale,
    out_grad,
):
    tokens = hidden.shape[1]
    local_docs = documents[0]
    dp_index = lax.axis_index("dp")
    mp_index = lax.axis_index("mp")
    row_docs = lax.all_gather(local_docs, "dp", axis=0, tiled=True)
    seq_len = row_docs.shape[0]
    query_place = dp_index * tokens + jnp.arange(tokens, dtype=jnp.int32)
    key_place = jnp.arange(seq_len, dtype=jnp.int32)
    visible = (local_docs[:, None] == row_docs[None, :]) & (
        key_place[None, :] <= query_place[:, None]
    )
    cosine, sine_val = rotary(positions[0])
    unit_count = w_up.shape[2]
    unit_start = mp_index * unit_count

    def fetch(layer_no):
        return (
            lax.all_gather(w_query[layer_no], ("dp", "mp"), axis=0, tiled=True),
            lax.all_gather(w_key[layer_no], ("dp", "mp"), axis=0, tiled=True),
            lax.all_gather(w_value[layer_no], ("dp", "mp"), axis=0, tiled=True),
            lax.all_gather(w_out[layer_no], ("dp", "mp"), axis=0, tiled=True),
        )

    def attention_part(stream, weights, layer_no):
        weight_q, weight_k, weight_v, weight_o = weights
        flat_b16 = stream.astype(jnp.bfloat16)
        q_raw = jnp.dot(flat_b16, weight_q, preferred_element_type=jnp.float32)
        k_raw = jnp.dot(flat_b16, weight_k, preferred_element_type=jnp.float32)
        v_raw = jnp.dot(flat_b16, weight_v, preferred_element_type=jnp.float32)
        q_turned = turn(q_raw, cosine, sine_val)
        k_turned = turn(k_raw, cosine, sine_val)
        q_unit = head_normed(q_turned)
        k_unit = head_normed(k_turned)
        queries = (qk_scale[layer_no] * q_unit).astype(jnp.bfloat16)
        key_vals = (qk_scale[layer_no] * k_unit).astype(jnp.bfloat16)
        value_vals = v_raw.astype(jnp.bfloat16)
        all_keys, all_values = (
            lax.all_gather(key_vals, "dp", axis=0, tiled=True),
            lax.all_gather(value_vals, "dp", axis=0, tiled=True),
        )
        mixture, log_total = attend_forward(queries, all_keys, all_values, visible)
        mixed_b16 = mixture.astype(jnp.bfloat16)
        projected = jnp.dot(mixed_b16, weight_o, preferred_element_type=jnp.float32)
        return {
            "flat": flat_b16,
            "q_turned": q_turned,
            "k_turned": k_turned,
            "q_unit": q_unit,
            "k_unit": k_unit,
            "queries": queries,
            "key_vals": key_vals,
            "value_vals": value_vals,
            "all_keys": all_keys,
            "all_values": all_values,
            "mixed": mixed_b16,
            "log_total": log_total,
            "projected": projected,
            "branch": normed(projected),
        }

    def mlp_part(middle, layer_no):
        flat_b16 = middle.astype(jnp.bfloat16)
        gathered = lax.all_gather(flat_b16, "mp", axis=0, tiled=True)
        up_pre = jnp.dot(gathered, w_up[layer_no], preferred_element_type=jnp.float32)
        gate_pre = jnp.dot(gathered, w_gate[layer_no], preferred_element_type=jnp.float32)
        factor_up = lax.dynamic_slice_in_dim(up_scale[layer_no], unit_start, unit_count)
        factor_gate = lax.dynamic_slice_in_dim(gate_scale[layer_no], unit_start, unit_count)
        up_val = factor_up * up_pre
        gate_val = factor_gate * gate_pre
        act_b16 = (up_val * jax.nn.silu(gate_val)).astype(jnp.bfloat16)
        down_sum = lax.psum_scatter(
            jnp.dot(act_b16, w_down[layer_no], preferred_element_type=jnp.float32).astype(
                jnp.bfloat16
            ),
            "mp",
            scatter_dimension=0,
            tiled=True,
        ).astype(jnp.float32)
        return {
            "gathered": gathered,
            "up_pre": up_pre,
            "gate_pre": gate_pre,
            "factor_up": factor_up,
            "factor_gate": factor_gate,
            "up_val": up_val,
            "gate_val": gate_val,
            "act": act_b16,
            "down_sum": down_sum,
            "branch": normed(down_sum),
        }

    def layer_forward(stream, weights, layer_no):
        attention = attention_part(stream, weights, layer_no)
        pre_mid = stream + attn_rate[layer_no] * (attention["branch"] - stream)
        middle = normed(pre_mid)
        feed = mlp_part(middle, layer_no)
        pre_out = middle + mlp_rate[layer_no] * (feed["branch"] - middle)
        return (attention, pre_mid, middle, feed, pre_out, normed(pre_out))

    stream = hidden[0]
    inputs = []
    kept_weights = []
    for layer_no in range(LAYERS):
        weights = fetch(layer_no)
        kept_weights.append(weights)
        inputs.append(stream)
        stream = layer_forward(stream, weights, layer_no)[5]
    output = stream
    grad_list = {
        "q": [None] * LAYERS,
        "k": [None] * LAYERS,
        "v": [None] * LAYERS,
        "o": [None] * LAYERS,
        "up": [None] * LAYERS,
        "gate": [None] * LAYERS,
        "down": [None] * LAYERS,
        "qk": [None] * LAYERS,
        "ra": [None] * LAYERS,
        "rm": [None] * LAYERS,
        "su": [None] * LAYERS,
        "sg": [None] * LAYERS,
    }
    stream_grad = out_grad[0]
    for layer_no in reversed(range(LAYERS)):
        weights = fetch(layer_no)
        weight_q, weight_k, weight_v, weight_o = weights
        stream = inputs[layer_no]
        attention, pre_mid, middle, feed, pre_out, result = layer_forward(stream, weights, layer_no)
        rate_mlp = mlp_rate[layer_no]
        rate_attn = attn_rate[layer_no]
        d_pre_out = norm_back(result, pre_out, stream_grad)
        grad_list["rm"][layer_no] = jnp.sum(d_pre_out * (feed["branch"] - middle), axis=0)
        d_down = norm_back(feed["branch"], feed["down_sum"], rate_mlp * d_pre_out).astype(
            jnp.bfloat16
        )
        d_middle = (1.0 - rate_mlp) * d_pre_out
        d_gathered = lax.all_gather(d_down, "mp", axis=0, tiled=True)
        d_act = contract_cols(d_gathered, w_down[layer_no])
        down_local = contract_rows(feed["act"], d_gathered)
        sigmoid_g = jax.nn.sigmoid(feed["gate_val"])
        d_up = d_act * jax.nn.silu(feed["gate_val"])
        d_gate = (
            d_act * feed["up_val"] * (sigmoid_g + feed["gate_val"] * sigmoid_g * (1.0 - sigmoid_g))
        )
        d_up_pre = (feed["factor_up"] * d_up).astype(jnp.bfloat16)
        d_gate_pre = (feed["factor_gate"] * d_gate).astype(jnp.bfloat16)
        zero_units = jnp.zeros((FF,), jnp.float32)
        grad_list["su"][layer_no] = lax.dynamic_update_slice_in_dim(
            zero_units, jnp.sum(feed["up_pre"] * d_up, axis=0), unit_start, 0
        )
        grad_list["sg"][layer_no] = lax.dynamic_update_slice_in_dim(
            zero_units, jnp.sum(feed["gate_pre"] * d_gate, axis=0), unit_start, 0
        )
        up_local = contract_rows(feed["gathered"], d_up_pre)
        gate_local = contract_rows(feed["gathered"], d_gate_pre)
        d_middle = d_middle + lax.psum_scatter(
            (
                contract_cols(d_up_pre, w_up[layer_no])
                + contract_cols(d_gate_pre, w_gate[layer_no])
            ).astype(jnp.bfloat16),
            "mp",
            scatter_dimension=0,
            tiled=True,
        ).astype(jnp.float32)
        up_shard, gate_shard, down_shard = (
            lax.psum_scatter(
                up_local.astype(jnp.bfloat16), "dp", scatter_dimension=0, tiled=True
            ).astype(jnp.float32),
            lax.psum_scatter(
                gate_local.astype(jnp.bfloat16), "dp", scatter_dimension=0, tiled=True
            ).astype(jnp.float32),
            lax.psum_scatter(
                down_local.astype(jnp.bfloat16), "dp", scatter_dimension=1, tiled=True
            ).astype(jnp.float32),
        )
        grad_list["up"][layer_no] = up_shard
        grad_list["gate"][layer_no] = gate_shard
        grad_list["down"][layer_no] = down_shard
        d_pre_mid = norm_back(middle, pre_mid, d_middle)
        grad_list["ra"][layer_no] = jnp.sum(d_pre_mid * (attention["branch"] - stream), axis=0)
        d_proj = norm_back(
            attention["branch"], attention["projected"], rate_attn * d_pre_mid
        ).astype(jnp.bfloat16)
        d_stream = (1.0 - rate_attn) * d_pre_mid
        out_local = contract_rows(attention["mixed"], d_proj)
        d_mixed = contract_cols(d_proj, weight_o).astype(jnp.bfloat16)
        d_query, d_key_all, d_value_all, row_inner = attend_back(
            attention["queries"], attention["all_keys"], attention["all_values"], d_mixed, visible
        )
        part_key = d_key_all.transpose(1, 0, 2).reshape(tokens * lax.axis_size("dp"), D)
        part_value = d_value_all.transpose(1, 0, 2).reshape(tokens * lax.axis_size("dp"), D)
        key_value = lax.psum_scatter(
            jnp.concatenate([part_key, part_value], axis=1).astype(jnp.bfloat16),
            "dp",
            scatter_dimension=0,
            tiled=True,
        ).astype(jnp.float32)
        d_key = key_value[:, :D]
        d_value = key_value[:, D:]
        factor_qk = qk_scale[layer_no]
        grad_list["qk"][layer_no] = jnp.sum(
            attention["q_unit"] * d_query + attention["k_unit"] * d_key, axis=0
        )
        d_q_raw = turn(
            head_norm_back(attention["q_unit"], attention["q_turned"], factor_qk * d_query),
            cosine,
            -sine_val,
        ).astype(jnp.bfloat16)
        d_k_raw = turn(
            head_norm_back(attention["k_unit"], attention["k_turned"], factor_qk * d_key),
            cosine,
            -sine_val,
        ).astype(jnp.bfloat16)
        d_v_raw = d_value.astype(jnp.bfloat16)
        flat_b16 = attention["flat"]
        q_local = contract_rows(flat_b16, d_q_raw)
        k_local = contract_rows(flat_b16, d_k_raw)
        v_local = contract_rows(flat_b16, d_v_raw)
        d_stream = (
            d_stream
            + contract_cols(d_q_raw, weight_q)
            + contract_cols(d_k_raw, weight_k)
            + contract_cols(d_v_raw, weight_v)
        )
        q_shard, k_shard, v_shard, o_shard = (
            lax.psum_scatter(q_local, ("dp", "mp"), scatter_dimension=0, tiled=True),
            lax.psum_scatter(k_local, ("dp", "mp"), scatter_dimension=0, tiled=True),
            lax.psum_scatter(v_local, ("dp", "mp"), scatter_dimension=0, tiled=True),
            lax.psum_scatter(out_local, ("dp", "mp"), scatter_dimension=0, tiled=True),
        )
        grad_list["q"][layer_no] = q_shard
        grad_list["k"][layer_no] = k_shard
        grad_list["v"][layer_no] = v_shard
        grad_list["o"][layer_no] = o_shard
        stream_grad = d_stream
    small_sums = lax.psum(
        (
            jnp.stack(grad_list["qk"]),
            jnp.stack(grad_list["ra"]),
            jnp.stack(grad_list["rm"]),
            jnp.stack(grad_list["su"]),
            jnp.stack(grad_list["sg"]),
        ),
        ("dp", "mp"),
    )
    return (
        output[None],
        stream_grad[None],
        jnp.stack(grad_list["q"]),
        jnp.stack(grad_list["k"]),
        jnp.stack(grad_list["v"]),
        jnp.stack(grad_list["o"]),
        small_sums[0],
        small_sums[1],
        small_sums[2],
        jnp.stack(grad_list["up"]),
        jnp.stack(grad_list["gate"]),
        jnp.stack(grad_list["down"]),
        small_sums[3],
        small_sums[4],
    )


SLOTS = (0, 2, 4, 6, 1, 3, 5, 7)
bf16 = jnp.bfloat16
f32 = jnp.float32


def swap(value, axis, bit):
    count = lax.axis_size(axis)
    return lax.ppermute(value, axis, [(j, j ^ bit) for j in range(count)])


def gather_row(block):
    half = block.shape[0] // 2
    along_x = swap(block, "dp", 2)
    along_y = swap(block, "dp", 4)
    corner = jnp.concatenate(
        [swap(along_x[:half], "dp", 4), swap(along_y[half:], "dp", 2)], axis=0
    )
    even = [block, along_x, along_y, corner]
    odd = [swap(part, "dp", 1) for part in even]
    return jnp.concatenate(even + odd, axis=0)


def scatter_row(partial):
    size = partial.shape[0] // 8
    half = size // 2
    other = swap(partial[4 * size :].astype(bf16), "dp", 1)
    even = partial[: 4 * size].astype(f32) + other.astype(f32)
    corner = even[3 * size :].astype(bf16)
    via_y = swap(corner[:half], "dp", 4)
    via_x = swap(corner[half:], "dp", 2)
    along_x = jnp.concatenate(
        [even[size : size + half] + via_y.astype(f32), even[size + half : 2 * size]], axis=0
    )
    along_y = jnp.concatenate(
        [even[2 * size : 2 * size + half], even[2 * size + half : 3 * size] + via_x.astype(f32)],
        axis=0,
    )
    from_x = swap(along_x.astype(bf16), "dp", 2)
    from_y = swap(along_y.astype(bf16), "dp", 4)
    return even[:size] + from_x.astype(f32) + from_y.astype(f32)


def gather_z(block):
    return jnp.concatenate([block] + [swap(block, "mp", k) for k in (1, 2, 3)], axis=0)


def scatter_z(blocks):
    got = [swap(blocks[k].astype(bf16), "mp", k).astype(f32) for k in (1, 2, 3)]
    return (blocks[0].astype(f32) + got[0]) + (got[1] + got[2])


def fast_device(
    hidden,
    documents,
    positions,
    w_query,
    w_key,
    w_value,
    w_out,
    qk_scale,
    attn_rate,
    mlp_rate,
    w_up,
    w_gate,
    w_down,
    up_scale,
    gate_scale,
    out_grad,
):
    tokens = hidden.shape[1]
    dp_index = lax.axis_index("dp")
    mp_index = lax.axis_index("mp")
    seq_len = 8 * tokens
    rows = w_query.shape[1]
    cols = D // 8
    local_heads = HEADS // 8
    order = jnp.array(SLOTS, jnp.int32) ^ dp_index

    tags = lax.all_gather(jnp.stack([documents[0], positions[0]]), "dp", axis=0, tiled=False)
    tags = jnp.take(tags, order, axis=0)
    row_docs = tags[:, 0].reshape(seq_len)
    row_pos = tags[:, 1].reshape(seq_len)
    place = (order[:, None] * tokens + jnp.arange(tokens, dtype=jnp.int32)[None, :]).reshape(seq_len)
    visible = (row_docs[:, None] == row_docs[None, :]) & (place[None, :] <= place[:, None])
    frequency = jnp.exp(
        jnp.arange(HEAD_DIM // 2, dtype=f32) * (-2.0 * math.log(10000.0) / HEAD_DIM)
    )
    angles = row_pos.astype(f32)[:, None] * frequency[None, :]
    cosine, sine = lax.optimization_barrier((jnp.cos(angles), jnp.sin(angles)))
    cosine = cosine[:, None, :]
    sine = sine[:, None, :]

    def heads_of(matrix):
        return matrix.reshape(matrix.shape[0], local_heads, HEAD_DIM)

    def flat_of(tensor):
        return tensor.reshape(tensor.shape[0], cols)

    def turned(matrix, sine_val):
        split = heads_of(matrix)
        lead = split[..., : HEAD_DIM // 2]
        trail = split[..., HEAD_DIM // 2 :]
        return flat_of(
            jnp.concatenate(
                [lead * cosine - trail * sine_val, trail * cosine + lead * sine_val], axis=-1
            )
        )

    def weights_in(layer_no):
        packed = jnp.stack([w_query[layer_no], w_key[layer_no], w_value[layer_no]])
        packed = packed.reshape(3, rows, 8, cols).transpose(2, 1, 0, 3)
        packed = lax.all_to_all(packed, "dp", 0, 0, tiled=True)
        packed = lax.all_gather(packed, "mp", axis=1, tiled=False)
        return packed.reshape(D, 3 * cols)

    w_in = [weights_in(layer_no) for layer_no in range(LAYERS)]
    w_proj = lax.all_gather(w_out, "mp", axis=1, tiled=True)

    unit_count = w_up.shape[2]
    unit_start = mp_index * unit_count
    scale_cols = lax.dynamic_slice_in_dim(qk_scale, dp_index * cols, cols, 1)
    up_cols = lax.dynamic_slice_in_dim(up_scale, unit_start, unit_count, 1)
    gate_cols = lax.dynamic_slice_in_dim(gate_scale, unit_start, unit_count, 1)

    def unit_norm(matrix):
        return flat_of(normed(heads_of(matrix)))

    def unit_back(result, vector, grad_in):
        return flat_of(norm_back(heads_of(result), heads_of(vector), heads_of(grad_in)))

    def by_head(matrix):
        return heads_of(matrix).transpose(1, 0, 2)

    def chances_of(queries, keys):
        scores = jnp.einsum("htd,hsd->hts", by_head(queries), by_head(keys), preferred_element_type=f32)
        scores = jnp.where(visible[None], scores * HEAD_DIM ** (-0.5), -jnp.inf)
        exponent = jnp.exp(scores - jnp.max(scores, axis=-1, keepdims=True))
        return exponent / jnp.sum(exponent, axis=-1, keepdims=True)

    def attention_forward(queries, keys, values):
        chances = chances_of(queries, keys)
        mixed = jnp.einsum(
            "hts,hsd->thd", chances.astype(bf16), by_head(values), preferred_element_type=f32
        )
        return flat_of(mixed).astype(bf16)

    def attention_back(queries, keys, values, d_mixed):
        chances = chances_of(queries, keys)
        d_chance = jnp.einsum("htd,hsd->hts", by_head(d_mixed), by_head(values), preferred_element_type=f32)
        inner = jnp.sum(chances * d_chance, axis=-1, keepdims=True)
        d_score = (chances * (d_chance - inner)).astype(bf16)
        d_query = jnp.einsum("hts,hsd->thd", d_score, by_head(keys), preferred_element_type=f32)
        d_key = jnp.einsum("hts,htd->shd", d_score, by_head(queries), preferred_element_type=f32)
        d_value = jnp.einsum(
            "hts,htd->shd", chances.astype(bf16), by_head(d_mixed), preferred_element_type=f32
        )
        scale = HEAD_DIM ** (-0.5)
        return flat_of(d_query) * scale, flat_of(d_key) * scale, flat_of(d_value)

    def forward(stream, layer_no):
        flat = gather_row(stream.astype(bf16))
        raw = jnp.dot(flat, w_in[layer_no], preferred_element_type=f32)
        q_turned = turned(raw[:, :cols], sine)
        k_turned = turned(raw[:, cols : 2 * cols], sine)
        values = raw[:, 2 * cols :].astype(bf16)
        q_unit = unit_norm(q_turned)
        k_unit = unit_norm(k_turned)
        queries = (scale_cols[layer_no] * q_unit).astype(bf16)
        keys = (scale_cols[layer_no] * k_unit).astype(bf16)
        mixed = attention_forward(queries, keys, values)
        projected = scatter_row(jnp.dot(mixed, w_proj[layer_no], preferred_element_type=f32))
        branch = normed(projected)
        pre_mid = stream + attn_rate[layer_no] * (branch - stream)
        middle = normed(pre_mid)
        gathered = gather_z(middle.astype(bf16))
        up_pre = jnp.dot(gathered, w_up[layer_no], preferred_element_type=f32)
        gate_pre = jnp.dot(gathered, w_gate[layer_no], preferred_element_type=f32)
        act = ((up_cols[layer_no] * up_pre) * jax.nn.silu(gate_cols[layer_no] * gate_pre)).astype(bf16)
        down = jnp.dot(act, w_down[layer_no], preferred_element_type=f32)
        down_sum = scatter_z([down[k * tokens : (k + 1) * tokens] for k in range(4)])
        mlp_branch = normed(down_sum)
        pre_out = middle + mlp_rate[layer_no] * (mlp_branch - middle)
        saved = dict(
            stream=stream, flat=flat, q_turned=q_turned, k_turned=k_turned, q_unit=q_unit,
            k_unit=k_unit, queries=queries, keys=keys, values=values, mixed=mixed,
            projected=projected, branch=branch, pre_mid=pre_mid, middle=middle, gathered=gathered,
            up_pre=up_pre, gate_pre=gate_pre, act=act, down_sum=down_sum, mlp_branch=mlp_branch,
            pre_out=pre_out,
        )
        saved["result"] = normed(pre_out)
        return saved

    def unit_grad(partial):
        return lax.psum_scatter(partial.astype(bf16), "dp", scatter_dimension=0, tiled=True).astype(f32)

    def backward(saved, grad, layer_no):
        rate_mlp = mlp_rate[layer_no]
        rate_attn = attn_rate[layer_no]
        d_pre_out = norm_back(saved["result"], saved["pre_out"], grad)
        out = {}
        out["rm"] = jnp.sum(d_pre_out * (saved["mlp_branch"] - saved["middle"]), axis=0)
        d_down = norm_back(saved["mlp_branch"], saved["down_sum"], rate_mlp * d_pre_out).astype(bf16)
        d_gathered = gather_z(d_down)
        d_act = contract_cols(d_gathered, w_down[layer_no])
        up_val = up_cols[layer_no] * saved["up_pre"]
        gate_val = gate_cols[layer_no] * saved["gate_pre"]
        sigmoid_g = jax.nn.sigmoid(gate_val)
        d_up = d_act * (gate_val * sigmoid_g)
        d_gate = d_act * up_val * (sigmoid_g + gate_val * sigmoid_g * (1.0 - sigmoid_g))
        d_up_pre = (up_cols[layer_no] * d_up).astype(bf16)
        d_gate_pre = (gate_cols[layer_no] * d_gate).astype(bf16)
        out["su"] = jnp.sum(saved["up_pre"] * d_up, axis=0)
        out["sg"] = jnp.sum(saved["gate_pre"] * d_gate, axis=0)
        d_mid = contract_cols(d_up_pre, w_up[layer_no]) + contract_cols(d_gate_pre, w_gate[layer_no])
        d_middle = (1.0 - rate_mlp) * d_pre_out + scatter_z(
            [d_mid[k * tokens : (k + 1) * tokens] for k in range(4)]
        )
        out["down"] = unit_grad(contract_rows(d_gathered, saved["act"])).T
        out["up"] = unit_grad(contract_rows(saved["gathered"], d_up_pre))
        out["gate"] = unit_grad(contract_rows(saved["gathered"], d_gate_pre))
        d_pre_mid = norm_back(saved["middle"], saved["pre_mid"], d_middle)
        out["ra"] = jnp.sum(d_pre_mid * (saved["branch"] - saved["stream"]), axis=0)
        d_proj = norm_back(saved["branch"], saved["projected"], rate_attn * d_pre_mid).astype(bf16)
        d_proj_row = gather_row(d_proj)
        d_mixed = contract_cols(d_proj_row, w_proj[layer_no]).astype(bf16)
        out_local = contract_rows(saved["mixed"], d_proj_row)
        d_query, d_key, d_value = attention_back(
            saved["queries"], saved["keys"], saved["values"], d_mixed
        )
        factor = scale_cols[layer_no]
        out["qk"] = jnp.sum(saved["q_unit"] * d_query + saved["k_unit"] * d_key, axis=0)
        d_q_raw = turned(unit_back(saved["q_unit"], saved["q_turned"], factor * d_query), -sine)
        d_k_raw = turned(unit_back(saved["k_unit"], saved["k_turned"], factor * d_key), -sine)
        d_raw = jnp.concatenate([d_q_raw.astype(bf16), d_k_raw.astype(bf16), d_value.astype(bf16)], axis=1)
        grad_in = (1.0 - rate_attn) * d_pre_mid + scatter_row(contract_cols(d_raw, w_in[layer_no]))
        in_local = contract_rows(saved["flat"], d_raw).reshape(8, 4, rows, 3 * cols)
        in_local = scatter_z(
            [lax.dynamic_index_in_dim(in_local, mp_index ^ k, 1, False) for k in range(4)]
        )
        in_cols = lax.all_to_all(in_local.astype(bf16), "dp", 0, 0, tiled=True).astype(f32)
        in_cols = in_cols.reshape(8, rows, 3, cols).transpose(2, 1, 0, 3).reshape(3, rows, D)
        out["q"], out["k"], out["v"] = in_cols[0], in_cols[1], in_cols[2]
        out_local = out_local.reshape(4, rows, D)
        out["o"] = scatter_z(
            [lax.dynamic_index_in_dim(out_local, mp_index ^ k, 0, False) for k in range(4)]
        )
        return out, grad_in

    stream = hidden[0]
    kept = []
    for layer_no in range(LAYERS):
        kept.append(forward(stream, layer_no))
        stream = kept[-1]["result"]
    output = stream
    grad = out_grad[0]
    grads = [None] * LAYERS
    for layer_no in reversed(range(LAYERS)):
        grads[layer_no], grad = backward(kept[layer_no], grad, layer_no)

    def stacked(name):
        return jnp.stack([grads[layer_no][name] for layer_no in range(LAYERS)])

    wide_qk = lax.dynamic_update_slice_in_dim(
        jnp.zeros((LAYERS, D), f32), stacked("qk"), dp_index * cols, 1
    )
    small = jnp.concatenate([wide_qk, stacked("ra"), stacked("rm"), stacked("su"), stacked("sg")], axis=0)
    for bit in (1, 2, 4):
        small = small + swap(small, "dp", bit)
    others = [small] + [swap(small, "mp", k) for k in (1, 2, 3)]
    summed = (others[0] + others[1]) + (others[2] + others[3])
    units = jnp.zeros((4, 2 * LAYERS, unit_count), f32)
    for k in range(4):
        units = lax.dynamic_update_slice_in_dim(
            units, others[k][None, 3 * LAYERS :], mp_index ^ k, 0
        )
    units = units.transpose(1, 0, 2).reshape(2 * LAYERS, FF)
    return (
        output[None],
        grad[None],
        stacked("q"),
        stacked("k"),
        stacked("v"),
        stacked("o"),
        summed[:LAYERS],
        summed[LAYERS : 2 * LAYERS],
        summed[2 * LAYERS : 3 * LAYERS],
        stacked("up"),
        stacked("gate"),
        stacked("down"),
        units[:LAYERS],
        units[LAYERS:],
    )


def solution(mesh):
    placed = (
        P("mp", "dp", None),
        P("mp", "dp"),
        P("mp", "dp"),
        P(None, ("dp", "mp"), None),
        P(None, ("dp", "mp"), None),
        P(None, ("dp", "mp"), None),
        P(None, ("dp", "mp"), None),
        P(),
        P(),
        P(),
        P(None, None, "mp"),
        P(None, None, "mp"),
        P(None, "mp", None),
        P(),
        P(),
        P("mp", "dp", None),
    )
    return jax.shard_map(
        fast_device if mesh.shape["dp"] == 8 and mesh.shape["mp"] == 4 else per_device,
        mesh=mesh,
        in_specs=placed,
        out_specs=(
            P("mp", "dp", None),
            P("mp", "dp", None),
            P(None, ("dp", "mp"), None),
            P(None, ("dp", "mp"), None),
            P(None, ("dp", "mp"), None),
            P(None, ("dp", "mp"), None),
            P(),
            P(),
            P(),
            P(None, "dp", "mp"),
            P(None, "dp", "mp"),
            P(None, "mp", "dp"),
            P(),
            P(),
        ),
        check_vma=False,
    )
```

```python
import math

import jax
import jax.numpy as jnp
from jax import lax
from jax.sharding import PartitionSpec as P

D = 1024
HEADS = 16
HEAD_DIM = 64
FF = 4096
LAYERS = 2


EPS = 1e-06


def normed(vector):
    return vector * lax.rsqrt(jnp.mean(vector * vector, axis=-1, keepdims=True) + EPS)


def norm_back(result, vector, grad_in):
    factor = lax.rsqrt(jnp.mean(vector * vector, axis=-1, keepdims=True) + EPS)
    return factor * (grad_in - result * jnp.mean(result * grad_in, axis=-1, keepdims=True))


def to_heads(matrix):
    return matrix.reshape(matrix.shape[0], HEADS, HEAD_DIM)


def from_heads(tensor):
    return tensor.reshape(tensor.shape[0], HEADS * HEAD_DIM)


def head_normed(vector):
    return from_heads(normed(to_heads(vector)))


def head_norm_back(result, vector, grad_in):
    return from_heads(norm_back(to_heads(result), to_heads(vector), to_heads(grad_in)))


def rotary(pos_row):
    half_dim = HEAD_DIM // 2
    frequency = jnp.exp(
        jnp.arange(half_dim, dtype=jnp.float32) * (-2.0 * math.log(10000.0) / HEAD_DIM)
    )
    angles = pos_row.astype(jnp.float32)[:, None] * frequency[None, :]
    return (jnp.cos(angles)[:, None, :], jnp.sin(angles)[:, None, :])


def turn(vector, cosine, sine_val):
    half_dim = HEAD_DIM // 2
    split = to_heads(vector)
    leading = split[..., :half_dim]
    trailing = split[..., half_dim:]
    return from_heads(
        jnp.concatenate(
            [leading * cosine - trailing * sine_val, trailing * cosine + leading * sine_val],
            axis=-1,
        )
    )


def head_cut(matrix, head_no):
    return lax.dynamic_slice_in_dim(matrix, head_no * HEAD_DIM, HEAD_DIM, 1)


def contract_rows(left, right):
    return lax.dot_general(
        left, right, (((0,), (0,)), ((), ())), preferred_element_type=jnp.float32
    )


def contract_cols(left, right):
    return lax.dot_general(
        left, right, (((1,), (1,)), ((), ())), preferred_element_type=jnp.float32
    )


def head_scores(query_head, key_head, visible):
    scores = jnp.einsum(
        "td,sd->ts", query_head, key_head, preferred_element_type=jnp.float32
    ) * HEAD_DIM ** (-0.5)
    return jnp.where(visible, scores, -jnp.inf)


def softmax_parts(scores):
    maximum = jnp.max(scores, axis=-1, keepdims=True)
    exponent = jnp.exp(scores - maximum)
    summed = jnp.sum(exponent, axis=-1, keepdims=True)
    return (exponent / summed, maximum[:, 0] + jnp.log(summed[:, 0]))


def attend_forward(queries, all_keys, all_values, visible):

    def one_head(head_no):
        chances, log_total = softmax_parts(
            head_scores(head_cut(queries, head_no), head_cut(all_keys, head_no), visible)
        )
        mixture = jnp.dot(
            chances.astype(jnp.bfloat16),
            head_cut(all_values, head_no),
            preferred_element_type=jnp.float32,
        )
        return (mixture, log_total)

    mixture, log_total = lax.map(one_head, jnp.arange(HEADS))
    return (from_heads(mixture.transpose(1, 0, 2)), log_total)


def attend_back(queries, all_keys, all_values, grad_mix, visible):

    def one_head(head_no):
        query_head = head_cut(queries, head_no)
        key_head = head_cut(all_keys, head_no)
        value_head = head_cut(all_values, head_no)
        grad_head = head_cut(grad_mix, head_no)
        chances, log_total = softmax_parts(head_scores(query_head, key_head, visible))
        d_chance = jnp.einsum(
            "td,sd->ts", grad_head, value_head, preferred_element_type=jnp.float32
        )
        row_inner = jnp.sum(chances * d_chance, axis=-1, keepdims=True)
        d_score = (chances * (d_chance - row_inner)).astype(jnp.bfloat16)
        d_query = jnp.dot(d_score, key_head, preferred_element_type=jnp.float32) * HEAD_DIM ** (
            -0.5
        )
        d_key = jnp.einsum(
            "ts,td->sd", d_score, query_head, preferred_element_type=jnp.float32
        ) * HEAD_DIM ** (-0.5)
        d_value = jnp.einsum(
            "ts,td->sd", chances.astype(jnp.bfloat16), grad_head, preferred_element_type=jnp.float32
        )
        return (d_query, d_key, d_value, row_inner[:, 0])

    d_query, d_key, d_value, row_inner = lax.map(one_head, jnp.arange(HEADS))
    return (from_heads(d_query.transpose(1, 0, 2)), d_key, d_value, row_inner)


def per_device(
    hidden,
    documents,
    positions,
    w_query,
    w_key,
    w_value,
    w_out,
    qk_scale,
    attn_rate,
    mlp_rate,
    w_up,
    w_gate,
    w_down,
    up_scale,
    gate_scale,
    out_grad,
):
    tokens = hidden.shape[1]
    local_docs = documents[0]
    dp_index = lax.axis_index("dp")
    mp_index = lax.axis_index("mp")
    row_docs = lax.all_gather(local_docs, "dp", axis=0, tiled=True)
    seq_len = row_docs.shape[0]
    query_place = dp_index * tokens + jnp.arange(tokens, dtype=jnp.int32)
    key_place = jnp.arange(seq_len, dtype=jnp.int32)
    visible = (local_docs[:, None] == row_docs[None, :]) & (
        key_place[None, :] <= query_place[:, None]
    )
    cosine, sine_val = rotary(positions[0])
    unit_count = w_up.shape[2]
    unit_start = mp_index * unit_count

    def fetch(layer_no):
        return (
            lax.all_gather(w_query[layer_no], ("dp", "mp"), axis=0, tiled=True),
            lax.all_gather(w_key[layer_no], ("dp", "mp"), axis=0, tiled=True),
            lax.all_gather(w_value[layer_no], ("dp", "mp"), axis=0, tiled=True),
            lax.all_gather(w_out[layer_no], ("dp", "mp"), axis=0, tiled=True),
        )

    def attention_part(stream, weights, layer_no):
        weight_q, weight_k, weight_v, weight_o = weights
        flat_b16 = stream.astype(jnp.bfloat16)
        q_raw = jnp.dot(flat_b16, weight_q, preferred_element_type=jnp.float32)
        k_raw = jnp.dot(flat_b16, weight_k, preferred_element_type=jnp.float32)
        v_raw = jnp.dot(flat_b16, weight_v, preferred_element_type=jnp.float32)
        q_turned = turn(q_raw, cosine, sine_val)
        k_turned = turn(k_raw, cosine, sine_val)
        q_unit = head_normed(q_turned)
        k_unit = head_normed(k_turned)
        queries = (qk_scale[layer_no] * q_unit).astype(jnp.bfloat16)
        key_vals = (qk_scale[layer_no] * k_unit).astype(jnp.bfloat16)
        value_vals = v_raw.astype(jnp.bfloat16)
        all_keys, all_values = (
            lax.all_gather(key_vals, "dp", axis=0, tiled=True),
            lax.all_gather(value_vals, "dp", axis=0, tiled=True),
        )
        mixture, log_total = attend_forward(queries, all_keys, all_values, visible)
        mixed_b16 = mixture.astype(jnp.bfloat16)
        projected = jnp.dot(mixed_b16, weight_o, preferred_element_type=jnp.float32)
        return {
            "flat": flat_b16,
            "q_turned": q_turned,
            "k_turned": k_turned,
            "q_unit": q_unit,
            "k_unit": k_unit,
            "queries": queries,
            "key_vals": key_vals,
            "value_vals": value_vals,
            "all_keys": all_keys,
            "all_values": all_values,
            "mixed": mixed_b16,
            "log_total": log_total,
            "projected": projected,
            "branch": normed(projected),
        }

    def mlp_part(middle, layer_no):
        flat_b16 = middle.astype(jnp.bfloat16)
        gathered = lax.all_gather(flat_b16, "mp", axis=0, tiled=True)
        up_pre = jnp.dot(gathered, w_up[layer_no], preferred_element_type=jnp.float32)
        gate_pre = jnp.dot(gathered, w_gate[layer_no], preferred_element_type=jnp.float32)
        factor_up = lax.dynamic_slice_in_dim(up_scale[layer_no], unit_start, unit_count)
        factor_gate = lax.dynamic_slice_in_dim(gate_scale[layer_no], unit_start, unit_count)
        up_val = factor_up * up_pre
        gate_val = factor_gate * gate_pre
        act_b16 = (up_val * jax.nn.silu(gate_val)).astype(jnp.bfloat16)
        down_sum = lax.psum_scatter(
            jnp.dot(act_b16, w_down[layer_no], preferred_element_type=jnp.float32).astype(
                jnp.bfloat16
            ),
            "mp",
            scatter_dimension=0,
            tiled=True,
        ).astype(jnp.float32)
        return {
            "gathered": gathered,
            "up_pre": up_pre,
            "gate_pre": gate_pre,
            "factor_up": factor_up,
            "factor_gate": factor_gate,
            "up_val": up_val,
            "gate_val": gate_val,
            "act": act_b16,
            "down_sum": down_sum,
            "branch": normed(down_sum),
        }

    def layer_forward(stream, weights, layer_no):
        attention = attention_part(stream, weights, layer_no)
        pre_mid = stream + attn_rate[layer_no] * (attention["branch"] - stream)
        middle = normed(pre_mid)
        feed = mlp_part(middle, layer_no)
        pre_out = middle + mlp_rate[layer_no] * (feed["branch"] - middle)
        return (attention, pre_mid, middle, feed, pre_out, normed(pre_out))

    stream = hidden[0]
    inputs = []
    kept_weights = []
    for layer_no in range(LAYERS):
        weights = fetch(layer_no)
        kept_weights.append(weights)
        inputs.append(stream)
        stream = layer_forward(stream, weights, layer_no)[5]
    output = stream
    grad_list = {
        "q": [None] * LAYERS,
        "k": [None] * LAYERS,
        "v": [None] * LAYERS,
        "o": [None] * LAYERS,
        "up": [None] * LAYERS,
        "gate": [None] * LAYERS,
        "down": [None] * LAYERS,
        "qk": [None] * LAYERS,
        "ra": [None] * LAYERS,
        "rm": [None] * LAYERS,
        "su": [None] * LAYERS,
        "sg": [None] * LAYERS,
    }
    stream_grad = out_grad[0]
    for layer_no in reversed(range(LAYERS)):
        weights = fetch(layer_no)
        weight_q, weight_k, weight_v, weight_o = weights
        stream = inputs[layer_no]
        attention, pre_mid, middle, feed, pre_out, result = layer_forward(stream, weights, layer_no)
        rate_mlp = mlp_rate[layer_no]
        rate_attn = attn_rate[layer_no]
        d_pre_out = norm_back(result, pre_out, stream_grad)
        grad_list["rm"][layer_no] = jnp.sum(d_pre_out * (feed["branch"] - middle), axis=0)
        d_down = norm_back(feed["branch"], feed["down_sum"], rate_mlp * d_pre_out).astype(
            jnp.bfloat16
        )
        d_middle = (1.0 - rate_mlp) * d_pre_out
        d_gathered = lax.all_gather(d_down, "mp", axis=0, tiled=True)
        d_act = contract_cols(d_gathered, w_down[layer_no])
        down_local = contract_rows(feed["act"], d_gathered)
        sigmoid_g = jax.nn.sigmoid(feed["gate_val"])
        d_up = d_act * jax.nn.silu(feed["gate_val"])
        d_gate = (
            d_act * feed["up_val"] * (sigmoid_g + feed["gate_val"] * sigmoid_g * (1.0 - sigmoid_g))
        )
        d_up_pre = (feed["factor_up"] * d_up).astype(jnp.bfloat16)
        d_gate_pre = (feed["factor_gate"] * d_gate).astype(jnp.bfloat16)
        zero_units = jnp.zeros((FF,), jnp.float32)
        grad_list["su"][layer_no] = lax.dynamic_update_slice_in_dim(
            zero_units, jnp.sum(feed["up_pre"] * d_up, axis=0), unit_start, 0
        )
        grad_list["sg"][layer_no] = lax.dynamic_update_slice_in_dim(
            zero_units, jnp.sum(feed["gate_pre"] * d_gate, axis=0), unit_start, 0
        )
        up_local = contract_rows(feed["gathered"], d_up_pre)
        gate_local = contract_rows(feed["gathered"], d_gate_pre)
        d_middle = d_middle + lax.psum_scatter(
            (
                contract_cols(d_up_pre, w_up[layer_no])
                + contract_cols(d_gate_pre, w_gate[layer_no])
            ).astype(jnp.bfloat16),
            "mp",
            scatter_dimension=0,
            tiled=True,
        ).astype(jnp.float32)
        up_shard, gate_shard, down_shard = (
            lax.psum_scatter(
                up_local.astype(jnp.bfloat16), "dp", scatter_dimension=0, tiled=True
            ).astype(jnp.float32),
            lax.psum_scatter(
                gate_local.astype(jnp.bfloat16), "dp", scatter_dimension=0, tiled=True
            ).astype(jnp.float32),
            lax.psum_scatter(
                down_local.astype(jnp.bfloat16), "dp", scatter_dimension=1, tiled=True
            ).astype(jnp.float32),
        )
        grad_list["up"][layer_no] = up_shard
        grad_list["gate"][layer_no] = gate_shard
        grad_list["down"][layer_no] = down_shard
        d_pre_mid = norm_back(middle, pre_mid, d_middle)
        grad_list["ra"][layer_no] = jnp.sum(d_pre_mid * (attention["branch"] - stream), axis=0)
        d_proj = norm_back(
            attention["branch"], attention["projected"], rate_attn * d_pre_mid
        ).astype(jnp.bfloat16)
        d_stream = (1.0 - rate_attn) * d_pre_mid
        out_local = contract_rows(attention["mixed"], d_proj)
        d_mixed = contract_cols(d_proj, weight_o).astype(jnp.bfloat16)
        d_query, d_key_all, d_value_all, row_inner = attend_back(
            attention["queries"], attention["all_keys"], attention["all_values"], d_mixed, visible
        )
        part_key = d_key_all.transpose(1, 0, 2).reshape(tokens * lax.axis_size("dp"), D)
        part_value = d_value_all.transpose(1, 0, 2).reshape(tokens * lax.axis_size("dp"), D)
        key_value = lax.psum_scatter(
            jnp.concatenate([part_key, part_value], axis=1).astype(jnp.bfloat16),
            "dp",
            scatter_dimension=0,
            tiled=True,
        ).astype(jnp.float32)
        d_key = key_value[:, :D]
        d_value = key_value[:, D:]
        factor_qk = qk_scale[layer_no]
        grad_list["qk"][layer_no] = jnp.sum(
            attention["q_unit"] * d_query + attention["k_unit"] * d_key, axis=0
        )
        d_q_raw = turn(
            head_norm_back(attention["q_unit"], attention["q_turned"], factor_qk * d_query),
            cosine,
            -sine_val,
        ).astype(jnp.bfloat16)
        d_k_raw = turn(
            head_norm_back(attention["k_unit"], attention["k_turned"], factor_qk * d_key),
            cosine,
            -sine_val,
        ).astype(jnp.bfloat16)
        d_v_raw = d_value.astype(jnp.bfloat16)
        flat_b16 = attention["flat"]
        q_local = contract_rows(flat_b16, d_q_raw)
        k_local = contract_rows(flat_b16, d_k_raw)
        v_local = contract_rows(flat_b16, d_v_raw)
        d_stream = (
            d_stream
            + contract_cols(d_q_raw, weight_q)
            + contract_cols(d_k_raw, weight_k)
            + contract_cols(d_v_raw, weight_v)
        )
        q_shard, k_shard, v_shard, o_shard = (
            lax.psum_scatter(q_local, ("dp", "mp"), scatter_dimension=0, tiled=True),
            lax.psum_scatter(k_local, ("dp", "mp"), scatter_dimension=0, tiled=True),
            lax.psum_scatter(v_local, ("dp", "mp"), scatter_dimension=0, tiled=True),
            lax.psum_scatter(out_local, ("dp", "mp"), scatter_dimension=0, tiled=True),
        )
        grad_list["q"][layer_no] = q_shard
        grad_list["k"][layer_no] = k_shard
        grad_list["v"][layer_no] = v_shard
        grad_list["o"][layer_no] = o_shard
        stream_grad = d_stream
    small_sums = lax.psum(
        (
            jnp.stack(grad_list["qk"]),
            jnp.stack(grad_list["ra"]),
            jnp.stack(grad_list["rm"]),
            jnp.stack(grad_list["su"]),
            jnp.stack(grad_list["sg"]),
        ),
        ("dp", "mp"),
    )
    return (
        output[None],
        stream_grad[None],
        jnp.stack(grad_list["q"]),
        jnp.stack(grad_list["k"]),
        jnp.stack(grad_list["v"]),
        jnp.stack(grad_list["o"]),
        small_sums[0],
        small_sums[1],
        small_sums[2],
        jnp.stack(grad_list["up"]),
        jnp.stack(grad_list["gate"]),
        jnp.stack(grad_list["down"]),
        small_sums[3],
        small_sums[4],
    )


SLOTS = (0, 2, 4, 6, 1, 3, 5, 7)
bf16 = jnp.bfloat16
f32 = jnp.float32


def swap(value, axis, bit):
    count = lax.axis_size(axis)
    return lax.ppermute(value, axis, [(j, j ^ bit) for j in range(count)])


def gather_row(block):
    half = block.shape[0] // 2
    along_x = swap(block, "dp", 2)
    along_y = swap(block, "dp", 4)
    corner = jnp.concatenate(
        [swap(along_x[:half], "dp", 4), swap(along_y[half:], "dp", 2)], axis=0
    )
    even = [block, along_x, along_y, corner]
    odd = [swap(part, "dp", 1) for part in even]
    return jnp.concatenate(even + odd, axis=0)


def scatter_row(partial):
    middle = partial.shape[0] // 2
    other = swap(partial[middle:].astype(bf16), "dp", 1)
    return scatter_chips(partial[:middle].astype(f32) + other.astype(f32))


def scatter_chips(even):
    size = even.shape[0] // 4
    half = size // 2
    corner = even[3 * size :].astype(bf16)
    via_y = swap(corner[:half], "dp", 4)
    via_x = swap(corner[half:], "dp", 2)
    along_x = jnp.concatenate(
        [even[size : size + half] + via_y.astype(f32), even[size + half : 2 * size]], axis=0
    )
    along_y = jnp.concatenate(
        [even[2 * size : 2 * size + half], even[2 * size + half : 3 * size] + via_x.astype(f32)],
        axis=0,
    )
    from_x = swap(along_x.astype(bf16), "dp", 2)
    from_y = swap(along_y.astype(bf16), "dp", 4)
    return even[:size] + from_x.astype(f32) + from_y.astype(f32)


def gather_z(block):
    return jnp.concatenate([block] + [swap(block, "mp", k) for k in (1, 2, 3)], axis=0)


def scatter_z(blocks):
    got = [swap(blocks[k].astype(bf16), "mp", k).astype(f32) for k in (1, 2, 3)]
    return (blocks[0].astype(f32) + got[0]) + (got[1] + got[2])


def fast_device(
    hidden,
    documents,
    positions,
    w_query,
    w_key,
    w_value,
    w_out,
    qk_scale,
    attn_rate,
    mlp_rate,
    w_up,
    w_gate,
    w_down,
    up_scale,
    gate_scale,
    out_grad,
):
    tokens = hidden.shape[1]
    dp_index = lax.axis_index("dp")
    mp_index = lax.axis_index("mp")
    seq_len = 8 * tokens
    rows = w_query.shape[1]
    cols = D // 8
    local_heads = HEADS // 8
    order = jnp.array(SLOTS, jnp.int32) ^ dp_index

    tags = jnp.stack([documents[0], positions[0]])[None]
    for bit in (2, 4, 1):
        tags = jnp.concatenate([tags, swap(tags, "dp", bit)], axis=0)
    row_docs = tags[:, 0].reshape(seq_len)
    row_pos = tags[:, 1].reshape(seq_len)
    place = (order[:, None] * tokens + jnp.arange(tokens, dtype=jnp.int32)[None, :]).reshape(seq_len)
    visible = (row_docs[:, None] == row_docs[None, :]) & (place[None, :] <= place[:, None])
    frequency = jnp.exp(
        jnp.arange(HEAD_DIM // 2, dtype=f32) * (-2.0 * math.log(10000.0) / HEAD_DIM)
    )
    angles = row_pos.astype(f32)[:, None] * frequency[None, :]
    cosine, sine = lax.optimization_barrier((jnp.cos(angles), jnp.sin(angles)))
    cosine = cosine[:, None, :]
    sine = sine[:, None, :]

    def heads_of(matrix):
        return matrix.reshape(matrix.shape[0], local_heads, HEAD_DIM)

    def flat_of(tensor):
        return tensor.reshape(tensor.shape[0], cols)

    def turned(matrix, sine_val):
        split = heads_of(matrix)
        lead = split[..., : HEAD_DIM // 2]
        trail = split[..., HEAD_DIM // 2 :]
        return flat_of(
            jnp.concatenate(
                [lead * cosine - trail * sine_val, trail * cosine + lead * sine_val], axis=-1
            )
        )

    def weights_in(layer_no):
        packed = jnp.stack([w_query[layer_no], w_key[layer_no], w_value[layer_no]])
        packed = packed.reshape(3, rows, 8, cols).transpose(2, 1, 0, 3)
        packed = lax.all_to_all(packed, "dp", 0, 0, tiled=True)
        if layer_no == 0:
            whole = jnp.zeros((8, 4, rows, 3, cols), bf16)
            for k in range(4):
                part = swap(packed, "mp", k) if k else packed
                whole = lax.dynamic_update_slice_in_dim(whole, part[:, None], mp_index ^ k, 1)
        else:
            whole = lax.all_gather(packed.reshape(8 * rows, 3 * cols), "mp", axis=0, tiled=True)
            whole = whole.reshape(4, 8, rows, 3 * cols).transpose(1, 0, 2, 3)
        return whole.reshape(D, 3 * cols)

    w_in = [weights_in(layer_no) for layer_no in range(LAYERS)]
    w_proj = [lax.all_gather(w_out[layer_no], "mp", axis=0, tiled=True) for layer_no in range(LAYERS)]

    unit_count = w_up.shape[2]
    unit_start = mp_index * unit_count
    scale_cols = lax.dynamic_slice_in_dim(qk_scale, dp_index * cols, cols, 1)
    up_cols = lax.dynamic_slice_in_dim(up_scale, unit_start, unit_count, 1)
    gate_cols = lax.dynamic_slice_in_dim(gate_scale, unit_start, unit_count, 1)

    def unit_norm(matrix):
        return flat_of(normed(heads_of(matrix)))

    def unit_back(result, vector, grad_in):
        return flat_of(norm_back(heads_of(result), heads_of(vector), heads_of(grad_in)))

    def by_head(matrix):
        return heads_of(matrix).transpose(1, 0, 2)

    def chances_of(queries, keys):
        scores = jnp.einsum("htd,hsd->hts", by_head(queries), by_head(keys), preferred_element_type=f32)
        scores = jnp.where(visible[None], scores * HEAD_DIM ** (-0.5), -jnp.inf)
        exponent = jnp.exp(scores - jnp.max(scores, axis=-1, keepdims=True))
        return exponent / jnp.sum(exponent, axis=-1, keepdims=True)

    def attention_forward(queries, keys, values):
        chances = chances_of(queries, keys)
        mixed = jnp.einsum(
            "hts,hsd->thd", chances.astype(bf16), by_head(values), preferred_element_type=f32
        )
        return flat_of(mixed).astype(bf16)

    def attention_back(queries, keys, values, d_mixed):
        chances = chances_of(queries, keys)
        d_chance = jnp.einsum("htd,hsd->hts", by_head(d_mixed), by_head(values), preferred_element_type=f32)
        inner = jnp.sum(chances * d_chance, axis=-1, keepdims=True)
        d_score = (chances * (d_chance - inner)).astype(bf16)
        d_query = jnp.einsum("hts,hsd->thd", d_score, by_head(keys), preferred_element_type=f32)
        d_key = jnp.einsum("hts,htd->shd", d_score, by_head(queries), preferred_element_type=f32)
        d_value = jnp.einsum(
            "hts,htd->shd", chances.astype(bf16), by_head(d_mixed), preferred_element_type=f32
        )
        scale = HEAD_DIM ** (-0.5)
        return flat_of(d_query) * scale, flat_of(d_key) * scale, flat_of(d_value)

    def forward(stream, layer_no):
        flat = gather_row(stream.astype(bf16))
        raw = jnp.dot(flat, w_in[layer_no], preferred_element_type=f32)
        q_turned = turned(raw[:, :cols], sine)
        k_turned = turned(raw[:, cols : 2 * cols], sine)
        values = raw[:, 2 * cols :].astype(bf16)
        q_unit = unit_norm(q_turned)
        k_unit = unit_norm(k_turned)
        queries = (scale_cols[layer_no] * q_unit).astype(bf16)
        keys = (scale_cols[layer_no] * k_unit).astype(bf16)
        mixed = attention_forward(queries, keys, values)
        projected = scatter_row(jnp.dot(mixed, w_proj[layer_no], preferred_element_type=f32))
        branch = normed(projected)
        pre_mid = stream + attn_rate[layer_no] * (branch - stream)
        middle = normed(pre_mid)
        gathered = gather_z(middle.astype(bf16))
        up_pre = jnp.dot(gathered, w_up[layer_no], preferred_element_type=f32)
        gate_pre = jnp.dot(gathered, w_gate[layer_no], preferred_element_type=f32)
        act = ((up_cols[layer_no] * up_pre) * jax.nn.silu(gate_cols[layer_no] * gate_pre)).astype(bf16)
        down = jnp.dot(act, w_down[layer_no], preferred_element_type=f32)
        down_sum = scatter_z([down[k * tokens : (k + 1) * tokens] for k in range(4)])
        mlp_branch = normed(down_sum)
        pre_out = middle + mlp_rate[layer_no] * (mlp_branch - middle)
        saved = dict(
            stream=stream, flat=flat, q_turned=q_turned, k_turned=k_turned, q_unit=q_unit,
            k_unit=k_unit, queries=queries, keys=keys, values=values, mixed=mixed,
            projected=projected, branch=branch, pre_mid=pre_mid, middle=middle, gathered=gathered,
            up_pre=up_pre, gate_pre=gate_pre, act=act, down_sum=down_sum, mlp_branch=mlp_branch,
            pre_out=pre_out,
        )
        saved["result"] = normed(pre_out)
        return saved

    def slot_cols(matrix, slots):
        return jnp.concatenate(
            [lax.dynamic_slice_in_dim(matrix, (dp_index ^ r) * cols, cols, 1) for r in slots], axis=1
        )

    def unit_grads(saved, d_gathered, d_units):
        pairs = ((saved["gathered"], d_units), (d_gathered, saved["act"]))
        odd = [contract_rows(slot_cols(x, SLOTS[4:]), y).astype(bf16) for x, y in pairs]
        odd = [swap(part, "dp", 1).astype(f32) for part in odd]
        even = [contract_rows(slot_cols(x, SLOTS[:4]), y) for x, y in pairs]
        return jnp.concatenate([even[0] + odd[0], even[1] + odd[1]], axis=1).astype(bf16)

    def weight_grads(in_local, out_local):
        in_local = in_local.reshape(8, 4, rows, 3 * cols)
        in_local = scatter_z(
            [lax.dynamic_index_in_dim(in_local, mp_index ^ k, 1, False) for k in range(4)]
        )
        in_cols = lax.all_to_all(in_local.astype(bf16), "dp", 0, 0, tiled=True).astype(f32)
        in_cols = in_cols.reshape(8, rows, 3, cols).transpose(2, 1, 0, 3).reshape(3, rows, D)
        out_local = out_local.reshape(4, rows, D)
        out_rows = scatter_z(
            [lax.dynamic_index_in_dim(out_local, mp_index ^ k, 0, False) for k in range(4)]
        )
        return {"q": in_cols[0], "k": in_cols[1], "v": in_cols[2], "o": out_rows}

    def backward(saved, grad, layer_no, pending):
        rate_mlp = mlp_rate[layer_no]
        rate_attn = attn_rate[layer_no]
        d_pre_out = norm_back(saved["result"], saved["pre_out"], grad)
        out = {}
        out["rm"] = jnp.sum(d_pre_out * (saved["mlp_branch"] - saved["middle"]), axis=0)
        d_down = norm_back(saved["mlp_branch"], saved["down_sum"], rate_mlp * d_pre_out).astype(bf16)
        d_gathered = gather_z(d_down)
        d_act = contract_cols(d_gathered, w_down[layer_no])
        up_val = up_cols[layer_no] * saved["up_pre"]
        gate_val = gate_cols[layer_no] * saved["gate_pre"]
        sigmoid_g = jax.nn.sigmoid(gate_val)
        d_up = d_act * (gate_val * sigmoid_g)
        d_gate = d_act * up_val * (sigmoid_g + gate_val * sigmoid_g * (1.0 - sigmoid_g))
        d_up_pre = (up_cols[layer_no] * d_up).astype(bf16)
        d_gate_pre = (gate_cols[layer_no] * d_gate).astype(bf16)
        out["su"] = jnp.sum(saved["up_pre"] * d_up, axis=0)
        out["sg"] = jnp.sum(saved["gate_pre"] * d_gate, axis=0)
        d_mid = contract_cols(d_up_pre, w_up[layer_no]) + contract_cols(d_gate_pre, w_gate[layer_no])
        d_middle = (1.0 - rate_mlp) * d_pre_out + scatter_z(
            [d_mid[k * tokens : (k + 1) * tokens] for k in range(4)]
        )
        chip_sums = unit_grads(saved, d_gathered, jnp.concatenate([d_up_pre, d_gate_pre], axis=1))
        d_pre_mid = norm_back(saved["middle"], saved["pre_mid"], d_middle)
        out["ra"] = jnp.sum(d_pre_mid * (saved["branch"] - saved["stream"]), axis=0)
        d_proj = norm_back(saved["branch"], saved["projected"], rate_attn * d_pre_mid).astype(bf16)
        d_proj, chip_sums = lax.optimization_barrier((d_proj, chip_sums))
        d_proj_row = gather_row(d_proj)
        units = scatter_chips(chip_sums.astype(f32))
        out["up"] = units[:, :unit_count]
        out["gate"] = units[:, unit_count : 2 * unit_count]
        out["down"] = units[:, 2 * unit_count :].T
        if pending is not None:
            d_proj_row, pending = lax.optimization_barrier((d_proj_row, pending))
            pending = weight_grads(*pending)
        d_mixed = contract_cols(d_proj_row, w_proj[layer_no]).astype(bf16)
        out_local = contract_rows(saved["mixed"], d_proj_row)
        d_query, d_key, d_value = attention_back(
            saved["queries"], saved["keys"], saved["values"], d_mixed
        )
        factor = scale_cols[layer_no]
        out["qk"] = jnp.sum(saved["q_unit"] * d_query + saved["k_unit"] * d_key, axis=0)
        d_q_raw = turned(unit_back(saved["q_unit"], saved["q_turned"], factor * d_query), -sine)
        d_k_raw = turned(unit_back(saved["k_unit"], saved["k_turned"], factor * d_key), -sine)
        d_raw = jnp.concatenate([d_q_raw.astype(bf16), d_k_raw.astype(bf16), d_value.astype(bf16)], axis=1)
        grad_in = (1.0 - rate_attn) * d_pre_mid + scatter_row(contract_cols(d_raw, w_in[layer_no]))
        return out, grad_in, pending, (contract_rows(saved["flat"], d_raw), out_local)

    stream = hidden[0]
    kept = []
    for layer_no in range(LAYERS):
        kept.append(forward(stream, layer_no))
        stream = kept[-1]["result"]
    output = stream
    grad = out_grad[0]
    grads = [None] * LAYERS
    pending = None
    for layer_no in reversed(range(LAYERS)):
        grads[layer_no], grad, done, pending = backward(kept[layer_no], grad, layer_no, pending)
        if done is not None:
            grads[layer_no + 1].update(done)
    grads[0].update(weight_grads(*pending))

    def stacked(name):
        return jnp.stack([grads[layer_no][name] for layer_no in range(LAYERS)])

    def sum_z(value):
        others = [value] + [swap(value, "mp", k) for k in (1, 2, 3)]
        return (others[0] + others[1]) + (others[2] + others[3]), others

    small = jnp.concatenate([stacked("ra"), stacked("rm"), stacked("su"), stacked("sg")], axis=0)
    for bit in (1, 2, 4):
        small = small + swap(small, "dp", bit)
    summed, others = sum_z(small)
    units = jnp.zeros((4, 2 * LAYERS, unit_count), f32)
    for k in range(4):
        units = lax.dynamic_update_slice_in_dim(
            units, others[k][None, 2 * LAYERS :], mp_index ^ k, 0
        )
    units = units.transpose(1, 0, 2).reshape(2 * LAYERS, FF)
    own_qk, _ = sum_z(stacked("qk"))
    wide_qk = lax.dynamic_update_slice_in_dim(
        jnp.zeros((LAYERS, D), f32), own_qk, dp_index * cols, 1
    )
    for bit in (1, 2, 4):
        wide_qk = wide_qk + swap(wide_qk, "dp", bit)
    return (
        output[None],
        grad[None],
        stacked("q"),
        stacked("k"),
        stacked("v"),
        stacked("o"),
        wide_qk,
        summed[:LAYERS],
        summed[LAYERS : 2 * LAYERS],
        stacked("up"),
        stacked("gate"),
        stacked("down"),
        units[:LAYERS],
        units[LAYERS:],
    )


def solution(mesh):
    placed = (
        P("mp", "dp", None),
        P("mp", "dp"),
        P("mp", "dp"),
        P(None, ("dp", "mp"), None),
        P(None, ("dp", "mp"), None),
        P(None, ("dp", "mp"), None),
        P(None, ("dp", "mp"), None),
        P(),
        P(),
        P(),
        P(None, None, "mp"),
        P(None, None, "mp"),
        P(None, "mp", None),
        P(),
        P(),
        P("mp", "dp", None),
    )
    return jax.shard_map(
        fast_device if mesh.shape["dp"] == 8 and mesh.shape["mp"] == 4 else per_device,
        mesh=mesh,
        in_specs=placed,
        out_specs=(
            P("mp", "dp", None),
            P("mp", "dp", None),
            P(None, ("dp", "mp"), None),
            P(None, ("dp", "mp"), None),
            P(None, ("dp", "mp"), None),
            P(None, ("dp", "mp"), None),
            P(),
            P(),
            P(),
            P(None, "dp", "mp"),
            P(None, "dp", "mp"),
            P(None, "mp", "dp"),
            P(),
            P(),
        ),
        check_vma=False,
    )
```
